32 devices in a mesh: tm: 8 (over z, x), col: 4 (over y, core).
Axes of the slice: x: 2, y: 2, z: 4, core: 2. Of those that a mesh axis runs over, the one named last changes fastest.
Arguments:
- design: float32 [4096, 32768], P('tm', 'col'), may hold values from -6 to 6
- fir_taps: float32 [128], replicated, may hold values from -0.5 to 0.5
- column_block: int32 [128], replicated, may hold values from 0 to 127, each once
- panels: int32 [2], replicated, may hold values from 0 to 127, as said below
Outputs:
- normal_rows: float32 [2, 256, 32768], P(None, 'tm', 'col')
The draws below stay inside these ranges and needn't reach their ends.
Inputs may be any that keep to these rules, and one draw needn't show every extreme that they name: column_block is a permutation of the block numbers. `panels`: the two entries differ; one of them is the last block number 128 - 1.
All inputs are finite; a program needn't handle non-finite values.
Results may differ from the reference program's by a relative error of at most 0.0001.
Values sent between devices are 32-bit elements; how exact they have to be, the bound alone decides.
A program may use at most 128 MiB of HBM per device.

```python
import jax
import jax.numpy as jnp
from jax import lax

NCOL = 32768
PANEL = 256
TAPS = 128
EPOCHS = 4096
NBLK = 128


def draw_panels(key, part):
    block_total = NCOL // PANEL
    top_block = jnp.full((), block_total - 1, jnp.int32)
    other_block = jax.random.randint(jax.random.fold_in(key, 7), (), 0, block_total - 1).astype(jnp.int32)
    slot_pick = jax.random.randint(jax.random.fold_in(key, 11), (), 0, 2).astype(jnp.int32)
    first = jnp.where(slot_pick == 0, top_block, other_block)
    second = jnp.where(slot_pick == 0, other_block, top_block)
    return jnp.stack([first, second]).astype(jnp.int32)


def block_scale(own_key, shape, cuts, least, high):
    def one(dim, shards_of):
        heights = jax.random.uniform(jax.random.fold_in(jax.random.fold_in(own_key, 6), dim), (shards_of,), jnp.float32, least / len(cuts), high / len(cuts))
        return jnp.repeat(jnp.exp(heights), shape[dim] // shards_of).reshape((-1,) + (1,) * (len(shape) - dim - 1))

    factor_of = one(*cuts[0])
    for cut in cuts[1:]:
        factor_of = factor_of * one(*cut)
    return factor_of


def scatter_about(rng, shape, scale, most, split=(), kind=jnp.bfloat16):
    gain = block_scale(rng, shape, split, -0.22, 0.18) if split else 1.0
    entries = jax.random.normal(rng, shape, jnp.float32) * scale * gain
    return jnp.minimum(jnp.maximum(entries, -most), most).astype(kind)


def setup_inputs(seed: int = 0) -> dict:
    key_of = jax.random.split(jax.random.key(seed), 5)
    return {
        "design": scatter_about(key_of[0], (EPOCHS, NCOL), 1.0, 6.0, ((0, 8), (1, 4)), jnp.float32),
        "fir_taps": scatter_about(key_of[1], (TAPS,), TAPS ** -0.5, 0.5, (), jnp.float32),
        "column_block": jax.random.permutation(key_of[2], NCOL // PANEL).astype(jnp.int32),
        "panels": draw_panels(jax.random.fold_in(key_of[4], 71), 0),
    }


def fir_matrices(fir_taps):
    tap_count = fir_taps.shape[0]
    lag_index = jnp.arange(tap_count, dtype=jnp.int32)[:, None] - jnp.arange(tap_count, dtype=jnp.int32)[None, :]
    current = jnp.where(lag_index >= 0, fir_taps[jnp.clip(lag_index, 0, tap_count - 1)], jnp.zeros((), fir_taps.dtype))
    previous = jnp.where(lag_index < 0, fir_taps[jnp.clip(lag_index + tap_count, 0, tap_count - 1)], jnp.zeros((), fir_taps.dtype))
    return previous, current


def reference(design, fir_taps, column_block, panels):
    row_count, col_width = design.shape
    previous, current = fir_matrices(fir_taps)
    extended = jnp.concatenate([jnp.zeros((TAPS, col_width), design.dtype), design], axis=0)
    extended = extended.reshape(row_count // TAPS + 1, TAPS, col_width)
    filtered = jnp.einsum("rs,bsc->brc", previous, extended[:-1], precision=lax.Precision.HIGHEST, preferred_element_type=jnp.float32)
    filtered = filtered + jnp.einsum("rs,bsc->brc", current, extended[1:], precision=lax.Precision.HIGHEST, preferred_element_type=jnp.float32)
    filtered = filtered.reshape(row_count, col_width)
    block_ids = jnp.arange(NBLK, dtype=jnp.int32)
    results = []
    for panel_slot in range(2):
        target = panels[panel_slot]
        position = jnp.sum(jnp.where(column_block == target, block_ids, 0)).astype(jnp.int32)
        panel_cols = lax.dynamic_slice_in_dim(filtered, (position * PANEL).astype(jnp.int32), PANEL, 1)
        gram = lax.dot_general(panel_cols, filtered, (((0,), (0,)), ((), ())), precision=lax.Precision.HIGHEST, preferred_element_type=jnp.float32)
        upper_mask = jnp.repeat((column_block >= target).astype(jnp.float32), PANEL)
        results.append(gram * upper_mask[None, :] / EPOCHS)
    return jnp.stack(results, axis=0)
```

```python
import functools

import jax
import jax.numpy as jnp
from jax import lax
from jax.experimental import pallas as pl
from jax.experimental.pallas import tpu as pltpu
from jax.sharding import PartitionSpec as P

PANEL = 256
STEP = 2
LAG = 4
EARLY = 3
MESH = pl.DeviceIdType.MESH
f32, bf16, i32 = jnp.float32, jnp.bfloat16, jnp.int32


def split(x):
    hi = x.astype(bf16)
    return hi, (x - hi.astype(f32)).astype(bf16)


def dot3(a, b):
    (ahi, alo), (bhi, blo) = a, b
    dot = functools.partial(jnp.dot, preferred_element_type=f32)
    return dot(ahi, bhi) + (dot(ahi, blo) + dot(alo, bhi))


def chunks_of(n):
    share = PANEL // n
    return 2 if share % 16 == 0 else 1


def prepare_kernel(
    groups, n, cb_hbm, panels_hbm, taps_hbm, d_hbm, cand_ref, last_ref, band_ref, index_ref, slot_ref, meta_ref,
    cb_ref, panels_ref, taps_ref, buf, sem,
):
    given = [
        pltpu.make_async_copy(src, dst, sem.at[2 + i])
        for i, (src, dst) in enumerate(((cb_hbm, cb_ref), (panels_hbm, panels_ref), (taps_hbm, taps_ref)))
    ]
    for copy in given:
        copy.start()
    total = cb_ref.shape[0]
    blocks = total // groups
    group = lax.axis_index("col")
    first = group * blocks
    for copy in given:
        copy.wait()
    jp = jnp.where(panels_ref[0] == total - 1, 1, 0)
    target = jnp.where(jp == 0, panels_ref[0], panels_ref[1])

    def find(i, carry):
        at, end = carry
        v = cb_ref[first + i]
        return jnp.where(v == target, i, at), jnp.where(v == total - 1, i, end)

    at, end = lax.fori_loop(0, blocks, find, (i32(-1), i32(-1)), unroll=8)

    def load(j, which):
        cols = pl.ds(pl.multiple_of(jnp.maximum(which, 0) * PANEL, PANEL), PANEL)
        return pltpu.make_async_copy(d_hbm.at[:, cols], buf.at[j], sem.at[j])

    load(0, at).start()
    load(1, end).start()

    most = i32(1)
    for g in range(groups):

        def tally(i, carry, g=g):
            v = cb_ref[g * blocks + i]
            return carry + jnp.where(v >= target, 1, 0) + jnp.where(v == total - 1, 1, 0)

        most = jnp.maximum(most, lax.fori_loop(0, blocks, tally, i32(0), unroll=8))

    @pl.loop(0, index_ref.shape[0])
    def _(s):
        index_ref[s] = 0

    def place(b, count):
        active = cb_ref[first + b] >= target
        index_ref[count] = b
        slot_ref[b] = jnp.where(active, count, -1)
        return count + jnp.where(active, 1, 0)

    count = lax.fori_loop(0, blocks, place, i32(0), unroll=4)
    index_ref[count] = jnp.where(end >= 0, blocks, 0)
    meta_ref[0] = most
    meta_ref[1] = jp
    meta_ref[2] = end
    meta_ref[3] = count

    taps = taps_ref.shape[1]
    line = jnp.concatenate([taps_ref[...], jnp.zeros_like(taps_ref)], axis=1)
    forward = pltpu.roll(jnp.broadcast_to(line, (2 * taps, 2 * taps)), taps, 1, stride=1, stride_axis=0)[:, :taps]
    adjoint = pltpu.roll(jnp.broadcast_to(line, (taps, 2 * taps)), 0, 1, stride=1, stride_axis=0).T
    band_ref[0], band_ref[1] = split(forward)
    band_ref[2], band_ref[3] = split(adjoint)

    load(0, at).wait()
    share = PANEL // n
    chunks = chunks_of(n)
    part = share // chunks
    block = jnp.where(at >= 0, buf[0], 0.0).T
    for h in range(chunks):
        for d in range(n):
            cand_ref[h, d * part : (d + 1) * part, :] = block[d * share + h * part : d * share + (h + 1) * part]
    load(1, end).wait()
    last_ref[...] = buf[1].T


def rows_kernel(
    levels, sides, count, index_ref, band_ref, cand_ref, last_ref, d_hbm, o_ref,
    d_ref, p_ref, whi_ref, wlo_ref, w_ref, mix_ref, sib_ref, far_ref, edge_ref, halo_ref, tail_ref, tailhalo_ref, *rest,
):
    bufs, sems = rest[:levels], rest[levels:]
    load_sem, send_sem, recv_sem, pre_send, pre_recv = sems
    blocks = d_ref.shape[0] - 1
    rows = d_ref.shape[1]
    taps = band_ref.shape[2]
    n = 1 << levels
    share = PANEL // n
    chunks = cand_ref.shape[0]
    part = share // chunks
    tall = PANEL // chunks
    half = tall // 2 if sides else tall
    units = chunks * count
    me = lax.axis_index("tm")
    col = lax.axis_index("col")
    bits = [(me // (1 << s)) % 2 for s in range(levels)]
    partners = [me + (1 - 2 * bits[s]) * (1 << s) for s in range(levels)]
    cbits = [(col // (1 << s)) % 2 for s in range(sides)]
    cpartners = [col + (1 - 2 * cbits[s]) * (1 << s) for s in range(sides)]
    has_before, has_after = me > 0, me < n - 1

    def load(c):
        cols = pl.ds(pl.multiple_of(c * PANEL, PANEL), PANEL)
        return pltpu.make_async_copy(d_hbm.at[:, cols], d_ref.at[c], load_sem.at[c])

    barrier = pltpu.get_barrier_semaphore()
    for s in range(levels):
        pl.semaphore_signal(barrier, inc=1, device_id={"tm": partners[s]}, device_id_type=MESH)
    for s in range(sides):
        pl.semaphore_signal(barrier, inc=1, device_id={"col": cpartners[s]}, device_id_type=MESH)

    @pl.when(has_after)
    def _():
        pl.semaphore_signal(barrier, inc=1, device_id={"tm": me + 1}, device_id_type=MESH)

    @pl.when(has_before)
    def _():
        pl.semaphore_signal(barrier, inc=1, device_id={"tm": me - 1}, device_id_type=MESH)

    @pl.loop(0, blocks)
    def _(c):
        load(c).start()

    tail_ref[...] = last_ref[:, rows - taps :]
    ends = jnp.where(has_after, 1, 0) + jnp.where(has_before, 1, 0)
    pl.semaphore_wait(barrier, levels + sides + ends)

    def remote(src, dst, k, where):
        return pltpu.make_async_remote_copy(
            src_ref=src, dst_ref=dst, send_sem=pre_send.at[k], recv_sem=pre_recv.at[k],
            device_id=where, device_id_type=MESH,
        )

    per = sides + 3
    mine = pl.ds(pl.multiple_of(cbits[0] * half, half), half) if sides else pl.ds(0, half)
    other = pl.ds(pl.multiple_of((1 - cbits[0]) * half, half), half) if sides else None

    def to_sibling(h):
        return remote(cand_ref.at[h, other], sib_ref.at[h], h * per, {"col": cpartners[0]})

    def to_far(h, s):
        return remote(mix_ref.at[h, s - 1], far_ref.at[h, s - 1], h * per + s, {"col": cpartners[s]})

    def to_after(h):
        return remote(edge_ref.at[h, 1], halo_ref.at[h, 0], h * per + sides, {"tm": me + 1})

    def from_before(h):
        return remote(edge_ref.at[h, 1], halo_ref.at[h, 0], h * per + sides, {"tm": me - 1})

    def to_before(h):
        return remote(edge_ref.at[h, 0], halo_ref.at[h, 1], h * per + sides + 1, {"tm": me - 1})

    def from_after(h):
        return remote(edge_ref.at[h, 0], halo_ref.at[h, 1], h * per + sides + 1, {"tm": me + 1})

    def give(h):
        return remote(w_ref.at[h, mine], w_ref.at[h, mine], h * per + sides + 2, {"col": cpartners[0]})

    def take(h):
        return remote(w_ref.at[h, other], w_ref.at[h, other], h * per + sides + 2, {"col": cpartners[0]})

    tail_at = chunks * per

    def tail_copy(where):
        return remote(tail_ref, tailhalo_ref, tail_at, {"tm": where})

    if sides:
        for h in range(chunks):
            to_sibling(h).start()

    @pl.when(has_after)
    def _():
        tail_copy(me + 1).start()

    for h in range(chunks):
        if sides:
            to_sibling(h).wait_recv()
            mix_ref[h, 0] = cand_ref[h, mine] + sib_ref[h]
        else:
            mix_ref[h, 0] = cand_ref[h]
        if sides > 1:
            to_far(h, 1).start()

    done = max(sides - 1, 0)

    def meet(h, s):
        to_far(h, s).wait_recv()
        mix_ref[h, s] = mix_ref[h, s - 1] + far_ref[h, s - 1]
        if s + 1 < sides:
            to_far(h, s + 1).start()

    def start_halo(h):
        edge_ref[h, 0] = mix_ref[h, done, :, :taps]
        edge_ref[h, 1] = mix_ref[h, done, :, rows - taps :]

        @pl.when(has_after)
        def _():
            to_after(h).start()

        @pl.when(has_before)
        def _():
            to_before(h).start()

    count_t = rows // taps

    def stacked(x, pieces):
        return jnp.concatenate([x[:, b * taps : (b + 2) * taps] for b in range(pieces)], axis=0)

    def unstacked(x, pieces):
        tall_ = x.shape[0] // pieces
        return jnp.concatenate([x[b * tall_ : (b + 1) * tall_] for b in range(pieces)], axis=1)

    def forward():
        return band_ref[0], band_ref[1]

    def adjoint():
        return band_ref[2], band_ref[3]

    def filter_last():
        @pl.when(has_before)
        def _():
            tail_copy(me - 1).wait_recv()

        @pl.when(jnp.logical_not(has_before))
        def _():
            tailhalo_ref[...] = jnp.zeros_like(tailhalo_ref)

        wide = max(taps, share)
        @pl.loop(0, PANEL // wide)
        def _(j):
            at = pl.ds(pl.multiple_of(j * wide, wide), wide)
            extended = jnp.concatenate([tailhalo_ref[at], last_ref[at]], axis=1)
            y_last = unstacked(dot3(split(stacked(extended, count_t)), forward()), count_t)
            d_ref[blocks, :, at] = y_last.T
            yhi, ylo = split(y_last)
            if chunks == 1:
                whi_ref[1, 0, at] = yhi
                wlo_ref[1, 0, at] = ylo
                return
            for h in range(chunks):
                for d in range(wide // share):
                    to = pl.ds(pl.multiple_of(j * (wide // chunks) + d * part, part), part)
                    rows_of = slice(d * share + h * part, d * share + (h + 1) * part)
                    whi_ref[1, h, to] = yhi[rows_of]
                    wlo_ref[1, h, to] = ylo[rows_of]

    def filter_chunk(h):
        @pl.when(has_before)
        def _():
            from_before(h).wait_recv()

        @pl.when(jnp.logical_not(has_before))
        def _():
            halo_ref[h, 0] = jnp.zeros_like(halo_ref[h, 0])

        @pl.when(has_after)
        def _():
            from_after(h).wait_recv()

        @pl.when(jnp.logical_not(has_after))
        def _():
            halo_ref[h, 1] = jnp.zeros_like(halo_ref[h, 1])

        whole = jnp.concatenate([halo_ref[h, 0], mix_ref[h, done], halo_ref[h, 1]], axis=1)
        y = unstacked(dot3(split(stacked(whole, count_t + 1)), forward()), count_t + 1)
        beyond = lax.broadcasted_iota(i32, y.shape, 1) >= jnp.where(has_after, rows + taps, rows)
        y = jnp.where(beyond, 0.0, y)
        w_ref[h, mine] = unstacked(dot3(split(stacked(y, count_t)), adjoint()), count_t)
        if sides:
            give(h).start()

    def ready_chunk(h):
        if sides:
            take(h).wait_recv()
        whi_ref[0, h], wlo_ref[0, h] = split(w_ref[h])

    def mixed(h):
        for s in range(1, sides):
            meet(h, s)
        start_halo(h)

    early = min(EARLY, count)

    mixed(0)
    filter_last()

    @pl.loop(0, blocks)
    def _(c):
        load(c).wait()

    def other_order(u):
        return (u % 4) // 3 if levels > 1 else 0

    def bit_of(s, u):
        if s > 1 or levels == 1:
            return bits[s], partners[s]
        swap = other_order(u)
        return (
            bits[s] + swap * (bits[1 - s] - bits[s]),
            partners[s] + swap * (partners[1 - s] - partners[s]),
        )

    def piece(s, u, bit):
        return (u,) + (slice(None),) * (levels - s - 1) + (bit,)

    def copy(s, u):
        src = p_ref if s == 0 else bufs[s - 1]
        bit, partner = bit_of(s, u)
        return pltpu.make_async_remote_copy(
            src_ref=src.at[piece(s, u, 1 - bit)],
            dst_ref=bufs[s].at[u],
            send_sem=send_sem.at[s, u],
            recv_sem=recv_sem.at[s, u],
            device_id={"tm": partner},
            device_id_type=MESH,
        )

    def compute(u):
        h, g = u // count, u % count
        d_at = index_ref[g]
        w_at = jnp.where(d_at == blocks, 1, 0)
        d_block = d_ref[d_at]
        value = dot3((whi_ref[w_at, h], wlo_ref[w_at, h]), split(d_block))
        for i in range(n):
            at = [(i >> s) & 1 for s in reversed(range(levels))]
            rows_of = value[i * part : (i + 1) * part]
            if levels == 1:
                p_ref[(u, *at)] = rows_of
                continue
            first, second = at[-2], at[-1]
            swap = other_order(u)
            p_ref[(u, *at[:-2], first + swap * (second - first), second + swap * (first - second))] = rows_of

    def add(s, u):
        copy(s, u).wait_recv()
        src = p_ref if s == 0 else bufs[s - 1]
        total = bufs[s][u] + src[piece(s, u, bit_of(s, u)[0])]
        if s == levels - 1:
            o_ref[u % count, u // count] = total
        else:
            bufs[s][u] = total
            copy(s + 1, u).start()

    def step(i):
        @pl.when(jnp.logical_and(i >= 0, i < units))
        def _():
            compute(i)
            copy(0, i).start()

        for s in range(levels):
            u = i - LAG * (s + 1)

            @pl.when(jnp.logical_and(u >= 0, u < units))
            def _():
                add(s, u)

    @pl.loop(-1, units + LAG * levels)
    def _(i):
        @pl.when(i == -1 if chunks == 1 else jnp.logical_or(i == -1, i == early))
        def _():
            h = jnp.where(i == early, 1, 0) if chunks > 1 else 0
            filter_chunk(h)
            if chunks > 1:

                @pl.when(i == -1)
                def _():
                    mixed(1)

            ready_chunk(h)

        step(i)

    for h in range(chunks):
        if sides:
            to_sibling(h).wait_send()
            give(h).wait_send()
        for s in range(1, sides):
            to_far(h, s).wait_send()

        @pl.when(has_after)
        def _():
            to_after(h).wait_send()

        @pl.when(has_before)
        def _():
            to_before(h).wait_send()

    @pl.when(has_after)
    def _():
        tail_copy(me + 1).wait_send()

    @pl.loop(0, units)
    def _(u):
        for s in range(levels):
            copy(s, u).wait_send()


def place_kernel(epochs, slot_ref, meta_ref, r_ref, o_hbm, o_ref, sem):
    blocks = slot_ref.shape[0]
    jp, end, gram = meta_ref[1], meta_ref[2], meta_ref[3]
    groups = sem.shape[0]
    per = blocks // groups

    def value(at):
        x = r_ref[at]
        return x.reshape(x.shape[0] * x.shape[1], x.shape[2]) / epochs

    def store(q):
        cols = pl.ds(pl.multiple_of(q * per * PANEL, PANEL), per * PANEL)
        return pltpu.make_async_copy(o_ref.at[:, :, cols], o_hbm.at[:, :, cols], sem.at[q])

    @pl.loop(0, groups)
    def _(q):
        for k in range(per):
            b = q * per + k
            cols = pl.ds(pl.multiple_of(b * PANEL, PANEL), PANEL)
            slot = slot_ref[b]
            o_ref[jp, :, cols] = jnp.where(slot >= 0, value(jnp.maximum(slot, 0)), 0.0)
            o_ref[1 - jp, :, cols] = jnp.where(end == b, value(jnp.where(end == b, gram, 0)), 0.0)
        store(q).start()

    @pl.loop(0, groups)
    def _(q):
        store(q).wait()


def vmem():
    return pl.BlockSpec(memory_space=pltpu.VMEM)


def smem():
    return pl.BlockSpec(memory_space=pltpu.SMEM)


def hbm():
    return pl.BlockSpec(memory_space=pl.ANY)


def params(**kw):
    return pltpu.CompilerParams(vmem_limit_bytes=56 * 2**20, **kw)


def summed_rows(count, index, band, cand, last, design, n, groups, cid):
    rows = design.shape[0]
    blocks = design.shape[1] // PANEL
    share = PANEL // n
    levels = n.bit_length() - 1
    sides = groups.bit_length() - 1
    chunks = chunks_of(n)
    part = share // chunks
    tall = PANEL // chunks
    half = tall // 2 if sides else tall
    units = chunks * count
    taps = band.shape[2]
    slots = blocks + 1
    copies = chunks * (sides + 3) + 1
    return pl.pallas_call(
        functools.partial(rows_kernel, levels, sides, count),
        out_shape=jax.ShapeDtypeStruct((slots, chunks, part, PANEL), f32),
        in_specs=[smem(), vmem(), vmem(), vmem(), hbm()],
        out_specs=vmem(),
        scratch_shapes=[
            pltpu.VMEM((blocks + 1, rows, PANEL), f32),
            pltpu.VMEM((units,) + (2,) * levels + (part, PANEL), f32),
            pltpu.VMEM((2, chunks, tall, rows), bf16),
            pltpu.VMEM((2, chunks, tall, rows), bf16),
            pltpu.VMEM((chunks, tall, rows), f32),
            pltpu.VMEM((chunks, max(sides, 1), half, rows), f32),
            pltpu.VMEM((chunks, half, rows), f32),
            pltpu.VMEM((chunks, max(sides - 1, 1), half, rows), f32),
            pltpu.VMEM((chunks, 2, half, taps), f32),
            pltpu.VMEM((chunks, 2, half, taps), f32),
            pltpu.VMEM((PANEL, taps), f32),
            pltpu.VMEM((PANEL, taps), f32),
        ]
        + [pltpu.VMEM((units,) + (2,) * (levels - s - 1) + (part, PANEL), f32) for s in range(levels)]
        + [
            pltpu.SemaphoreType.DMA((blocks,)),
            pltpu.SemaphoreType.DMA((levels, units)),
            pltpu.SemaphoreType.DMA((levels, units)),
            pltpu.SemaphoreType.DMA((copies,)),
            pltpu.SemaphoreType.DMA((copies,)),
        ],
        compiler_params=params(collective_id=cid, has_side_effects=True),
        name=f"rows_{count}",
    )(index, band, cand, last, design)


def shards(design, fir_taps, column_block, panels):
    rows, width = design.shape
    taps = fir_taps.shape[0]
    blocks = width // PANEL
    n = lax.axis_size("tm")
    groups = lax.axis_size("col")
    epochs = rows * n
    chunks = chunks_of(n)
    slots = blocks + 1

    cand, last, band, index, slot, meta = pl.pallas_call(
        functools.partial(prepare_kernel, groups, n),
        out_shape=(
            jax.ShapeDtypeStruct((chunks, PANEL // chunks, rows), f32),
            jax.ShapeDtypeStruct((PANEL, rows), f32),
            jax.ShapeDtypeStruct((4, 2 * taps, taps), bf16),
            jax.ShapeDtypeStruct((slots + 1,), i32),
            jax.ShapeDtypeStruct((blocks,), i32),
            jax.ShapeDtypeStruct((4,), i32),
        ),
        in_specs=[hbm()] * 4,
        out_specs=(vmem(), vmem(), vmem(), smem(), smem(), smem()),
        scratch_shapes=[
            pltpu.SMEM(column_block.shape, i32),
            pltpu.SMEM(panels.shape, i32),
            pltpu.VMEM((1, taps), f32),
            pltpu.VMEM((2, rows, PANEL), f32),
            pltpu.SemaphoreType.DMA((5,)),
        ],
        compiler_params=pltpu.CompilerParams(vmem_limit_bytes=8 * 2**20),
        name="prepare",
    )(column_block, panels, fir_taps.reshape(1, taps), design)
    counts = sorted({min(c, slots) for c in range(STEP, slots + STEP, STEP)})

    def branch(order, count, index, band, cand, last, design):
        return summed_rows(count, index, band, cand, last, design, n, groups, order)

    pick = jnp.clip((meta[0] + STEP - 1) // STEP - 1, 0, len(counts) - 1)
    own_rows = lax.switch(
        pick,
        [functools.partial(branch, i, c) for i, c in enumerate(counts)],
        index, band, cand, last, design,
    )
    return pl.pallas_call(
        functools.partial(place_kernel, epochs),
        out_shape=jax.ShapeDtypeStruct((2, PANEL // n, width), f32),
        in_specs=[smem(), smem(), vmem()],
        out_specs=hbm(),
        scratch_shapes=[pltpu.VMEM((2, PANEL // n, width), f32), pltpu.SemaphoreType.DMA((8 if blocks % 8 == 0 else blocks,))],
        compiler_params=pltpu.CompilerParams(vmem_limit_bytes=8 * 2**20),
        name="place",
    )(slot, meta, own_rows)


def solution(mesh):
    return jax.shard_map(
        shards,
        mesh=mesh,
        in_specs=(P("tm", "col"), P(), P(), P()),
        out_specs=P(None, "tm", "col"),
        check_vma=False,
    )
```

```python
import functools

import jax
import jax.numpy as jnp
from jax import lax
from jax.experimental import pallas as pl
from jax.experimental.pallas import tpu as pltpu
from jax.sharding import PartitionSpec as P

PANEL = 256
STEP = 2
LAG = 4
EARLY = 3
MOVED = 2
MESH = pl.DeviceIdType.MESH
f32, bf16, i32 = jnp.float32, jnp.bfloat16, jnp.int32


def split(x):
    hi = x.astype(bf16)
    return hi, (x - hi.astype(f32)).astype(bf16)


def dot3(a, b):
    (ahi, alo), (bhi, blo) = a, b
    dot = functools.partial(jnp.dot, preferred_element_type=f32)
    return dot(ahi, bhi) + (dot(ahi, blo) + dot(alo, bhi))


def chunks_of(n):
    share = PANEL // n
    return 2 if share % 16 == 0 else 1


def prepare_kernel(
    groups, n, cb_hbm, panels_hbm, taps_hbm, d_hbm, cand_ref, last_ref, band_ref, moved_hbm, index_ref, slot_ref, meta_ref,
    cb_ref, panels_ref, taps_ref, moved_ref, buf, sem,
):
    given = [
        pltpu.make_async_copy(src, dst, sem.at[2 + i])
        for i, (src, dst) in enumerate(((cb_hbm, cb_ref), (panels_hbm, panels_ref), (taps_hbm, taps_ref)))
    ]
    for copy in given:
        copy.start()
    total = cb_ref.shape[0]
    blocks = total // groups
    group = lax.axis_index("col")
    first = group * blocks
    for copy in given:
        copy.wait()
    jp = jnp.where(panels_ref[0] == total - 1, 1, 0)
    target = jnp.where(jp == 0, panels_ref[0], panels_ref[1])

    def find(i, carry):
        at, end = carry
        v = cb_ref[first + i]
        return jnp.where(v == target, i, at), jnp.where(v == total - 1, i, end)

    at, end = lax.fori_loop(0, blocks, find, (i32(-1), i32(-1)), unroll=8)

    def load(j, which):
        cols = pl.ds(pl.multiple_of(jnp.maximum(which, 0) * PANEL, PANEL), PANEL)
        return pltpu.make_async_copy(d_hbm.at[:, cols], buf.at[j], sem.at[j])

    load(0, at).start()
    load(1, end).start()

    def tally(i, carry):
        values = [cb_ref[g * blocks + i] for g in range(groups)]
        return tuple(
            c + jnp.where(v >= target, 1, 0) + jnp.where(v == total - 1, 1, 0) for c, v in zip(carry, values)
        )

    tallies = lax.fori_loop(0, blocks, tally, (i32(0),) * groups, unroll=8)
    most, leave, arrive = i32(1), i32(0), i32(0)
    for g in range(groups):
        here, there = tallies[g], tallies[g ^ 1]
        out = jnp.minimum(jnp.maximum(here - there, 0) // 2, MOVED)
        into = jnp.minimum(jnp.maximum(there - here, 0) // 2, MOVED)
        most = jnp.maximum(most, here - out + into)
        leave = jnp.where(group == g, out, leave)
        arrive = jnp.where(group == g, into, arrive)

    slots = blocks + 1
    spare = index_ref.shape[0] - 1

    @pl.loop(0, spare)
    def _(s):
        index_ref[s] = 0

    for j in range(MOVED):
        index_ref[j] = jnp.where(j < arrive, blocks + 1 + j, 0)
        moved_ref[j] = 0

    def place(b, count):
        active = cb_ref[first + b] >= target
        away = count < leave
        slot = arrive + count - leave
        moved_ref[jnp.where(away, count, MOVED)] = b
        index_ref[jnp.where(away, spare, slot)] = b
        slot_ref[b] = jnp.where(active, jnp.where(away, slots + count, slot), -1)
        return count + jnp.where(active, 1, 0)

    count = arrive - leave + lax.fori_loop(0, blocks, place, i32(0), unroll=4)
    index_ref[count] = jnp.where(end >= 0, blocks, 0)
    meta_ref[0] = most
    meta_ref[1] = jp
    meta_ref[2] = end
    meta_ref[3] = count

    def move(j):
        cols = pl.ds(pl.multiple_of(moved_ref[j] * PANEL, PANEL), PANEL)
        return pltpu.make_async_copy(d_hbm.at[:, cols], moved_hbm.at[j], sem.at[5 + j])

    for j in range(MOVED):
        move(j).start()

    taps = taps_ref.shape[1]
    line = jnp.concatenate([taps_ref[...], jnp.zeros_like(taps_ref)], axis=1)
    forward = pltpu.roll(jnp.broadcast_to(line, (2 * taps, 2 * taps)), taps, 1, stride=1, stride_axis=0)[:, :taps]
    adjoint = pltpu.roll(jnp.broadcast_to(line, (taps, 2 * taps)), 0, 1, stride=1, stride_axis=0).T
    band_ref[0], band_ref[1] = split(forward)
    band_ref[2], band_ref[3] = split(adjoint)

    load(0, at).wait()
    share = PANEL // n
    chunks = chunks_of(n)
    part = share // chunks
    block = jnp.where(at >= 0, buf[0], 0.0).T
    for h in range(chunks):
        for d in range(n):
            cand_ref[h, d * part : (d + 1) * part, :] = block[d * share + h * part : d * share + (h + 1) * part]
    load(1, end).wait()
    last_ref[...] = buf[1].T
    for j in range(MOVED):
        move(j).wait()


def rows_kernel(
    levels, sides, count, index_ref, band_ref, cand_ref, last_ref, moved_hbm, d_hbm, o_ref,
    d_ref, p_ref, whi_ref, wlo_ref, w_ref, mix_ref, sib_ref, far_ref, edge_ref, halo_ref, tail_ref, tailhalo_ref, back_ref, *rest,
):
    bufs, sems = rest[:levels], rest[levels:]
    load_sem, send_sem, recv_sem, pre_send, pre_recv = sems
    blocks = d_ref.shape[0] - 1 - MOVED
    rows = d_ref.shape[1]
    taps = band_ref.shape[2]
    n = 1 << levels
    share = PANEL // n
    chunks = cand_ref.shape[0]
    part = share // chunks
    tall = PANEL // chunks
    half = tall // 2 if sides else tall
    units = chunks * count
    me = lax.axis_index("tm")
    col = lax.axis_index("col")
    bits = [(me // (1 << s)) % 2 for s in range(levels)]
    partners = [me + (1 - 2 * bits[s]) * (1 << s) for s in range(levels)]
    cbits = [(col // (1 << s)) % 2 for s in range(sides)]
    cpartners = [col + (1 - 2 * cbits[s]) * (1 << s) for s in range(sides)]
    has_before, has_after = me > 0, me < n - 1

    def load(c):
        cols = pl.ds(pl.multiple_of(c * PANEL, PANEL), PANEL)
        return pltpu.make_async_copy(d_hbm.at[:, cols], d_ref.at[c], load_sem.at[c])

    barrier = pltpu.get_barrier_semaphore()
    for s in range(levels):
        pl.semaphore_signal(barrier, inc=1, device_id={"tm": partners[s]}, device_id_type=MESH)
    for s in range(sides):
        pl.semaphore_signal(barrier, inc=1, device_id={"col": cpartners[s]}, device_id_type=MESH)

    @pl.when(has_after)
    def _():
        pl.semaphore_signal(barrier, inc=1, device_id={"tm": me + 1}, device_id_type=MESH)

    @pl.when(has_before)
    def _():
        pl.semaphore_signal(barrier, inc=1, device_id={"tm": me - 1}, device_id_type=MESH)

    @pl.loop(0, blocks)
    def _(c):
        load(c).start()

    tail_ref[...] = last_ref[:, rows - taps :]
    ends = jnp.where(has_after, 1, 0) + jnp.where(has_before, 1, 0)
    pl.semaphore_wait(barrier, levels + sides + ends)

    def remote(src, dst, k, where):
        return pltpu.make_async_remote_copy(
            src_ref=src, dst_ref=dst, send_sem=pre_send.at[k], recv_sem=pre_recv.at[k],
            device_id=where, device_id_type=MESH,
        )

    per = sides + 3
    mine = pl.ds(pl.multiple_of(cbits[0] * half, half), half) if sides else pl.ds(0, half)
    other = pl.ds(pl.multiple_of((1 - cbits[0]) * half, half), half) if sides else None

    def to_sibling(h):
        return remote(cand_ref.at[h, other], sib_ref.at[h], h * per, {"col": cpartners[0]})

    def to_far(h, s):
        return remote(mix_ref.at[h, s - 1], far_ref.at[h, s - 1], h * per + s, {"col": cpartners[s]})

    def to_after(h):
        return remote(edge_ref.at[h, 1], halo_ref.at[h, 0], h * per + sides, {"tm": me + 1})

    def from_before(h):
        return remote(edge_ref.at[h, 1], halo_ref.at[h, 0], h * per + sides, {"tm": me - 1})

    def to_before(h):
        return remote(edge_ref.at[h, 0], halo_ref.at[h, 1], h * per + sides + 1, {"tm": me - 1})

    def from_after(h):
        return remote(edge_ref.at[h, 0], halo_ref.at[h, 1], h * per + sides + 1, {"tm": me + 1})

    def give(h):
        return remote(w_ref.at[h, mine], w_ref.at[h, mine], h * per + sides + 2, {"col": cpartners[0]})

    def take(h):
        return remote(w_ref.at[h, other], w_ref.at[h, other], h * per + sides + 2, {"col": cpartners[0]})

    tail_at = chunks * per

    def tail_copy(where):
        return remote(tail_ref, tailhalo_ref, tail_at, {"tm": where})

    def lend(j):
        return remote(moved_hbm.at[j], d_ref.at[blocks + 1 + j], tail_at + 1 + j, {"col": cpartners[0]})

    def give_back(j):
        return remote(o_ref.at[j], back_ref.at[j], tail_at + 1 + MOVED + j, {"col": cpartners[0]})

    if sides:
        for h in range(chunks):
            to_sibling(h).start()

    @pl.when(has_after)
    def _():
        tail_copy(me + 1).start()

    for j in range(MOVED):
        lend(j).start()

    for h in range(chunks):
        if sides:
            to_sibling(h).wait_recv()
            mix_ref[h, 0] = cand_ref[h, mine] + sib_ref[h]
        else:
            mix_ref[h, 0] = cand_ref[h]
        if sides > 1:
            to_far(h, 1).start()

    done = max(sides - 1, 0)

    def meet(h, s):
        to_far(h, s).wait_recv()
        mix_ref[h, s] = mix_ref[h, s - 1] + far_ref[h, s - 1]
        if s + 1 < sides:
            to_far(h, s + 1).start()

    def start_halo(h):
        edge_ref[h, 0] = mix_ref[h, done, :, :taps]
        edge_ref[h, 1] = mix_ref[h, done, :, rows - taps :]

        @pl.when(has_after)
        def _():
            to_after(h).start()

        @pl.when(has_before)
        def _():
            to_before(h).start()

    count_t = rows // taps

    def stacked(x, pieces):
        return jnp.concatenate([x[:, b * taps : (b + 2) * taps] for b in range(pieces)], axis=0)

    def unstacked(x, pieces):
        tall_ = x.shape[0] // pieces
        return jnp.concatenate([x[b * tall_ : (b + 1) * tall_] for b in range(pieces)], axis=1)

    def forward():
        return band_ref[0], band_ref[1]

    def adjoint():
        return band_ref[2], band_ref[3]

    def filter_last():
        @pl.when(has_before)
        def _():
            tail_copy(me - 1).wait_recv()

        @pl.when(jnp.logical_not(has_before))
        def _():
            tailhalo_ref[...] = jnp.zeros_like(tailhalo_ref)

        wide = max(taps, share)
        @pl.loop(0, PANEL // wide)
        def _(j):
            at = pl.ds(pl.multiple_of(j * wide, wide), wide)
            extended = jnp.concatenate([tailhalo_ref[at], last_ref[at]], axis=1)
            y_last = unstacked(dot3(split(stacked(extended, count_t)), forward()), count_t)
            d_ref[blocks, :, at] = y_last.T
            yhi, ylo = split(y_last)
            if chunks == 1:
                whi_ref[1, 0, at] = yhi
                wlo_ref[1, 0, at] = ylo
                return
            for h in range(chunks):
                for d in range(wide // share):
                    to = pl.ds(pl.multiple_of(j * (wide // chunks) + d * part, part), part)
                    rows_of = slice(d * share + h * part, d * share + (h + 1) * part)
                    whi_ref[1, h, to] = yhi[rows_of]
                    wlo_ref[1, h, to] = ylo[rows_of]

    def filter_chunk(h):
        @pl.when(has_before)
        def _():
            from_before(h).wait_recv()

        @pl.when(jnp.logical_not(has_before))
        def _():
            halo_ref[h, 0] = jnp.zeros_like(halo_ref[h, 0])

        @pl.when(has_after)
        def _():
            from_after(h).wait_recv()

        @pl.when(jnp.logical_not(has_after))
        def _():
            halo_ref[h, 1] = jnp.zeros_like(halo_ref[h, 1])

        whole = jnp.concatenate([halo_ref[h, 0], mix_ref[h, done], halo_ref[h, 1]], axis=1)
        y = unstacked(dot3(split(stacked(whole, count_t + 1)), forward()), count_t + 1)
        beyond = lax.broadcasted_iota(i32, y.shape, 1) >= jnp.where(has_after, rows + taps, rows)
        y = jnp.where(beyond, 0.0, y)
        w_ref[h, mine] = unstacked(dot3(split(stacked(y, count_t)), adjoint()), count_t)
        if sides:
            give(h).start()

    def ready_chunk(h):
        if sides:
            take(h).wait_recv()
        whi_ref[0, h], wlo_ref[0, h] = split(w_ref[h])

    def mixed(h):
        for s in range(1, sides):
            meet(h, s)
        start_halo(h)

    early = min(EARLY, count)

    mixed(0)
    filter_last()

    @pl.loop(0, blocks)
    def _(c):
        load(c).wait()

    for j in range(MOVED):
        lend(j).wait_recv()

    def other_order(u):
        return (u % 4) // 3 if levels > 1 else 0

    def bit_of(s, u):
        if s > 1 or levels == 1:
            return bits[s], partners[s]
        swap = other_order(u)
        return (
            bits[s] + swap * (bits[1 - s] - bits[s]),
            partners[s] + swap * (partners[1 - s] - partners[s]),
        )

    def piece(s, u, bit):
        return (u,) + (slice(None),) * (levels - s - 1) + (bit,)

    def copy(s, u):
        src = p_ref if s == 0 else bufs[s - 1]
        bit, partner = bit_of(s, u)
        return pltpu.make_async_remote_copy(
            src_ref=src.at[piece(s, u, 1 - bit)],
            dst_ref=bufs[s].at[u],
            send_sem=send_sem.at[s, u],
            recv_sem=recv_sem.at[s, u],
            device_id={"tm": partner},
            device_id_type=MESH,
        )

    def compute(u):
        h, g = u // count, u % count
        d_at = index_ref[g]
        w_at = jnp.where(d_at == blocks, 1, 0)
        d_block = d_ref[d_at]
        value = dot3((whi_ref[w_at, h], wlo_ref[w_at, h]), split(d_block))
        for i in range(n):
            at = [(i >> s) & 1 for s in reversed(range(levels))]
            rows_of = value[i * part : (i + 1) * part]
            if levels == 1:
                p_ref[(u, *at)] = rows_of
                continue
            first, second = at[-2], at[-1]
            swap = other_order(u)
            p_ref[(u, *at[:-2], first + swap * (second - first), second + swap * (first - second))] = rows_of

    def add(s, u):
        copy(s, u).wait_recv()
        src = p_ref if s == 0 else bufs[s - 1]
        total = bufs[s][u] + src[piece(s, u, bit_of(s, u)[0])]
        if s == levels - 1:
            o_ref[u % count, u // count] = total
            lent = u - (chunks - 1) * count

            @pl.when(jnp.logical_and(lent >= 0, lent < MOVED))
            def _():
                give_back(lent).start()

        else:
            bufs[s][u] = total
            copy(s + 1, u).start()

    def step(i):
        @pl.when(jnp.logical_and(i >= 0, i < units))
        def _():
            compute(i)
            copy(0, i).start()

        for s in range(levels):
            u = i - LAG * (s + 1)

            @pl.when(jnp.logical_and(u >= 0, u < units))
            def _():
                add(s, u)

    @pl.loop(-1, units + LAG * levels)
    def _(i):
        @pl.when(i == -1 if chunks == 1 else jnp.logical_or(i == -1, i == early))
        def _():
            h = jnp.where(i == early, 1, 0) if chunks > 1 else 0
            filter_chunk(h)
            if chunks > 1:

                @pl.when(i == -1)
                def _():
                    mixed(1)

            ready_chunk(h)

        step(i)

    for h in range(chunks):
        if sides:
            to_sibling(h).wait_send()
            give(h).wait_send()
        for s in range(1, sides):
            to_far(h, s).wait_send()

        @pl.when(has_after)
        def _():
            to_after(h).wait_send()

        @pl.when(has_before)
        def _():
            to_before(h).wait_send()

    @pl.when(has_after)
    def _():
        tail_copy(me + 1).wait_send()

    @pl.loop(0, units)
    def _(u):
        for s in range(levels):
            copy(s, u).wait_send()

    for j in range(MOVED):
        lend(j).wait_send()
        give_back(j).wait()
        o_ref[blocks + 1 + j] = back_ref[j]


def place_kernel(epochs, slot_ref, meta_ref, r_ref, o_hbm, o_ref, sem):
    blocks = slot_ref.shape[0]
    jp, end, gram = meta_ref[1], meta_ref[2], meta_ref[3]
    groups = sem.shape[0]
    per = blocks // groups

    def value(at):
        x = r_ref[at]
        return x.reshape(x.shape[0] * x.shape[1], x.shape[2]) / epochs

    def store(q):
        cols = pl.ds(pl.multiple_of(q * per * PANEL, PANEL), per * PANEL)
        return pltpu.make_async_copy(o_ref.at[:, :, cols], o_hbm.at[:, :, cols], sem.at[q])

    @pl.loop(0, groups)
    def _(q):
        for k in range(per):
            b = q * per + k
            cols = pl.ds(pl.multiple_of(b * PANEL, PANEL), PANEL)
            slot = slot_ref[b]
            o_ref[jp, :, cols] = jnp.where(slot >= 0, value(jnp.maximum(slot, 0)), 0.0)
            o_ref[1 - jp, :, cols] = jnp.where(end == b, value(jnp.where(end == b, gram, 0)), 0.0)
        store(q).start()

    @pl.loop(0, groups)
    def _(q):
        store(q).wait()


def vmem():
    return pl.BlockSpec(memory_space=pltpu.VMEM)


def smem():
    return pl.BlockSpec(memory_space=pltpu.SMEM)


def hbm():
    return pl.BlockSpec(memory_space=pl.ANY)


def params(**kw):
    return pltpu.CompilerParams(vmem_limit_bytes=56 * 2**20, **kw)


def summed_rows(count, index, band, cand, last, moved, design, n, groups, cid):
    rows = design.shape[0]
    blocks = design.shape[1] // PANEL
    share = PANEL // n
    levels = n.bit_length() - 1
    sides = groups.bit_length() - 1
    chunks = chunks_of(n)
    part = share // chunks
    tall = PANEL // chunks
    half = tall // 2 if sides else tall
    units = chunks * count
    taps = band.shape[2]
    slots = blocks + 1
    copies = chunks * (sides + 3) + 1 + 2 * MOVED
    return pl.pallas_call(
        functools.partial(rows_kernel, levels, sides, count),
        out_shape=jax.ShapeDtypeStruct((slots + MOVED, chunks, part, PANEL), f32),
        in_specs=[smem(), vmem(), vmem(), vmem(), hbm(), hbm()],
        out_specs=vmem(),
        scratch_shapes=[
            pltpu.VMEM((blocks + 1 + MOVED, rows, PANEL), f32),
            pltpu.VMEM((units,) + (2,) * levels + (part, PANEL), f32),
            pltpu.VMEM((2, chunks, tall, rows), bf16),
            pltpu.VMEM((2, chunks, tall, rows), bf16),
            pltpu.VMEM((chunks, tall, rows), f32),
            pltpu.VMEM((chunks, max(sides, 1), half, rows), f32),
            pltpu.VMEM((chunks, half, rows), f32),
            pltpu.VMEM((chunks, max(sides - 1, 1), half, rows), f32),
            pltpu.VMEM((chunks, 2, half, taps), f32),
            pltpu.VMEM((chunks, 2, half, taps), f32),
            pltpu.VMEM((PANEL, taps), f32),
            pltpu.VMEM((PANEL, taps), f32),
            pltpu.VMEM((MOVED, chunks, part, PANEL), f32),
        ]
        + [pltpu.VMEM((units,) + (2,) * (levels - s - 1) + (part, PANEL), f32) for s in range(levels)]
        + [
            pltpu.SemaphoreType.DMA((blocks,)),
            pltpu.SemaphoreType.DMA((levels, units)),
            pltpu.SemaphoreType.DMA((levels, units)),
            pltpu.SemaphoreType.DMA((copies,)),
            pltpu.SemaphoreType.DMA((copies,)),
        ],
        compiler_params=params(collective_id=cid, has_side_effects=True),
        name=f"rows_{count}",
    )(index, band, cand, last, moved, design)


def shards(design, fir_taps, column_block, panels):
    rows, width = design.shape
    taps = fir_taps.shape[0]
    blocks = width // PANEL
    n = lax.axis_size("tm")
    groups = lax.axis_size("col")
    epochs = rows * n
    chunks = chunks_of(n)
    slots = blocks + 1

    cand, last, band, moved, index, slot, meta = pl.pallas_call(
        functools.partial(prepare_kernel, groups, n),
        out_shape=(
            jax.ShapeDtypeStruct((chunks, PANEL // chunks, rows), f32),
            jax.ShapeDtypeStruct((PANEL, rows), f32),
            jax.ShapeDtypeStruct((4, 2 * taps, taps), bf16),
            jax.ShapeDtypeStruct((MOVED, rows, PANEL), f32),
            jax.ShapeDtypeStruct((slots + 2,), i32),
            jax.ShapeDtypeStruct((blocks,), i32),
            jax.ShapeDtypeStruct((4,), i32),
        ),
        in_specs=[hbm()] * 4,
        out_specs=(vmem(), vmem(), vmem(), hbm(), smem(), smem(), smem()),
        scratch_shapes=[
            pltpu.SMEM(column_block.shape, i32),
            pltpu.SMEM(panels.shape, i32),
            pltpu.VMEM((1, taps), f32),
            pltpu.SMEM((MOVED + 1,), i32),
            pltpu.VMEM((2, rows, PANEL), f32),
            pltpu.SemaphoreType.DMA((5 + MOVED,)),
        ],
        compiler_params=pltpu.CompilerParams(vmem_limit_bytes=60 * 2**20),
        name="prepare",
    )(column_block, panels, fir_taps.reshape(1, taps), design)
    counts = sorted({min(c, slots) for c in range(STEP, slots + STEP, STEP)})

    def branch(order, count, *operands):
        return summed_rows(count, *operands, n, groups, order)

    pick = jnp.clip((meta[0] + STEP - 1) // STEP - 1, 0, len(counts) - 1)
    own_rows = lax.switch(
        pick,
        [functools.partial(branch, i, c) for i, c in enumerate(counts)],
        index, band, cand, last, moved, design,
    )
    return pl.pallas_call(
        functools.partial(place_kernel, epochs),
        out_shape=jax.ShapeDtypeStruct((2, PANEL // n, width), f32),
        in_specs=[smem(), smem(), vmem()],
        out_specs=hbm(),
        scratch_shapes=[pltpu.VMEM((2, PANEL // n, width), f32), pltpu.SemaphoreType.DMA((8 if blocks % 8 == 0 else blocks,))],
        compiler_params=pltpu.CompilerParams(vmem_limit_bytes=8 * 2**20),
        name="place",
    )(slot, meta, own_rows)


def solution(mesh):
    return jax.shard_map(
        shards,
        mesh=mesh,
        in_specs=(P("tm", "col"), P(), P(), P()),
        out_specs=P(None, "tm", "col"),
        check_vma=False,
    )
```

```python
import functools

import jax
import jax.numpy as jnp
from jax import lax
from jax.experimental import pallas as pl
from jax.experimental.pallas import tpu as pltpu
from jax.sharding import PartitionSpec as P

PANEL = 256
STEP = 2
LAG = 4
EARLY = 3
MOVED = 2
MESH = pl.DeviceIdType.MESH
f32, bf16, i32 = jnp.float32, jnp.bfloat16, jnp.int32


def split(x):
    hi = x.astype(bf16)
    return hi, (x - hi.astype(f32)).astype(bf16)


def dot3(a, b):
    (ahi, alo), (bhi, blo) = a, b
    dot = functools.partial(jnp.dot, preferred_element_type=f32)
    return dot(ahi, bhi) + (dot(ahi, blo) + dot(alo, bhi))


def chunks_of(n):
    share = PANEL // n
    return 2 if share % 16 == 0 else 1


def prepare_kernel(
    groups, n, cb_hbm, panels_hbm, taps_hbm, d_hbm, cand_ref, last_ref, band_ref, moved_hbm, index_ref, slot_ref, meta_ref,
    cb_ref, panels_ref, taps_ref, moved_ref, buf, sem,
):
    given = [
        pltpu.make_async_copy(src, dst, sem.at[2 + i])
        for i, (src, dst) in enumerate(((cb_hbm, cb_ref), (panels_hbm, panels_ref), (taps_hbm, taps_ref)))
    ]
    for copy in given:
        copy.start()
    total = cb_ref.shape[0]
    blocks = total // groups
    group = lax.axis_index("col")
    first = group * blocks
    for copy in given:
        copy.wait()
    jp = jnp.where(panels_ref[0] == total - 1, 1, 0)
    target = jnp.where(jp == 0, panels_ref[0], panels_ref[1])

    def find(i, carry):
        at, end = carry
        v = cb_ref[first + i]
        return jnp.where(v == target, i, at), jnp.where(v == total - 1, i, end)

    at, end = lax.fori_loop(0, blocks, find, (i32(-1), i32(-1)), unroll=8)

    def load(j, which):
        cols = pl.ds(pl.multiple_of(jnp.maximum(which, 0) * PANEL, PANEL), PANEL)
        return pltpu.make_async_copy(d_hbm.at[:, cols], buf.at[j], sem.at[j])

    load(0, at).start()
    load(1, end).start()

    def tally(i, carry):
        values = [cb_ref[g * blocks + i] for g in range(groups)]
        return tuple(
            c + jnp.where(v >= target, 1, 0) + jnp.where(v == total - 1, 1, 0) for c, v in zip(carry, values)
        )

    tallies = lax.fori_loop(0, blocks, tally, (i32(0),) * groups, unroll=8)
    most, leave, arrive = i32(1), i32(0), i32(0)
    for g in range(groups):
        here, there = tallies[g], tallies[g ^ 1]
        out = jnp.minimum(jnp.maximum(here - there, 0) // 2, MOVED)
        into = jnp.minimum(jnp.maximum(there - here, 0) // 2, MOVED)
        most = jnp.maximum(most, here - out + into)
        leave = jnp.where(group == g, out, leave)
        arrive = jnp.where(group == g, into, arrive)

    slots = blocks + 1
    spare = index_ref.shape[0] - 1

    @pl.loop(0, spare)
    def _(s):
        index_ref[s] = 0

    for j in range(MOVED):
        index_ref[j] = jnp.where(j < arrive, blocks + 1 + j, 0)
        moved_ref[j] = 0

    def place(b, count):
        active = cb_ref[first + b] >= target
        away = count < leave
        slot = arrive + count - leave
        moved_ref[jnp.where(away, count, MOVED)] = b
        index_ref[jnp.where(away, spare, slot)] = b
        slot_ref[b] = jnp.where(active, jnp.where(away, slots + count, slot), -1)
        return count + jnp.where(active, 1, 0)

    count = arrive - leave + lax.fori_loop(0, blocks, place, i32(0), unroll=4)
    index_ref[count] = jnp.where(end >= 0, blocks, 0)
    meta_ref[0] = most
    meta_ref[1] = jp
    meta_ref[2] = end
    meta_ref[3] = count

    def move(j):
        cols = pl.ds(pl.multiple_of(moved_ref[j] * PANEL, PANEL), PANEL)
        return pltpu.make_async_copy(d_hbm.at[:, cols], moved_hbm.at[j], sem.at[5 + j])

    for j in range(MOVED):

        @pl.when(j < leave)
        def _():
            move(j).start()

    taps = taps_ref.shape[1]
    line = jnp.concatenate([taps_ref[...], jnp.zeros_like(taps_ref)], axis=1)
    forward = pltpu.roll(jnp.broadcast_to(line, (2 * taps, 2 * taps)), taps, 1, stride=1, stride_axis=0)[:, :taps]
    adjoint = pltpu.roll(jnp.broadcast_to(line, (taps, 2 * taps)), 0, 1, stride=1, stride_axis=0).T
    band_ref[0], band_ref[1] = split(forward)
    band_ref[2], band_ref[3] = split(adjoint)

    load(0, at).wait()
    share = PANEL // n
    chunks = chunks_of(n)
    part = share // chunks
    block = jnp.where(at >= 0, buf[0], 0.0).T
    for h in range(chunks):
        for d in range(n):
            cand_ref[h, d * part : (d + 1) * part, :] = block[d * share + h * part : d * share + (h + 1) * part]
    load(1, end).wait()
    last_ref[...] = buf[1].T
    for j in range(MOVED):

        @pl.when(j < leave)
        def _():
            move(j).wait()


def rows_kernel(
    levels, sides, count, index_ref, band_ref, cand_ref, last_ref, moved_hbm, d_hbm, o_ref,
    d_ref, p_ref, whi_ref, wlo_ref, w_ref, mix_ref, sib_ref, far_ref, edge_ref, halo_ref, tail_ref, tailhalo_ref, back_ref, *rest,
):
    bufs, sems = rest[:levels], rest[levels:]
    load_sem, send_sem, recv_sem, pre_send, pre_recv = sems
    blocks = d_ref.shape[0] - 1 - MOVED
    rows = d_ref.shape[1]
    taps = band_ref.shape[2]
    n = 1 << levels
    share = PANEL // n
    chunks = cand_ref.shape[0]
    part = share // chunks
    tall = PANEL // chunks
    half = tall // 2 if sides else tall
    units = chunks * count
    me = lax.axis_index("tm")
    col = lax.axis_index("col")
    bits = [(me // (1 << s)) % 2 for s in range(levels)]
    partners = [me + (1 - 2 * bits[s]) * (1 << s) for s in range(levels)]
    cbits = [(col // (1 << s)) % 2 for s in range(sides)]
    cpartners = [col + (1 - 2 * cbits[s]) * (1 << s) for s in range(sides)]
    has_before, has_after = me > 0, me < n - 1

    def load(c):
        cols = pl.ds(pl.multiple_of(c * PANEL, PANEL), PANEL)
        return pltpu.make_async_copy(d_hbm.at[:, cols], d_ref.at[c], load_sem.at[c])

    barrier = pltpu.get_barrier_semaphore()
    for s in range(levels):
        pl.semaphore_signal(barrier, inc=1, device_id={"tm": partners[s]}, device_id_type=MESH)
    for s in range(sides):
        pl.semaphore_signal(barrier, inc=1, device_id={"col": cpartners[s]}, device_id_type=MESH)

    @pl.when(has_after)
    def _():
        pl.semaphore_signal(barrier, inc=1, device_id={"tm": me + 1}, device_id_type=MESH)

    @pl.when(has_before)
    def _():
        pl.semaphore_signal(barrier, inc=1, device_id={"tm": me - 1}, device_id_type=MESH)

    @pl.loop(0, blocks)
    def _(c):
        load(c).start()

    tail_ref[...] = last_ref[:, rows - taps :]
    ends = jnp.where(has_after, 1, 0) + jnp.where(has_before, 1, 0)
    pl.semaphore_wait(barrier, levels + sides + ends)

    def remote(src, dst, k, where):
        return pltpu.make_async_remote_copy(
            src_ref=src, dst_ref=dst, send_sem=pre_send.at[k], recv_sem=pre_recv.at[k],
            device_id=where, device_id_type=MESH,
        )

    per = sides + 3
    mine = pl.ds(pl.multiple_of(cbits[0] * half, half), half) if sides else pl.ds(0, half)
    other = pl.ds(pl.multiple_of((1 - cbits[0]) * half, half), half) if sides else None

    def to_sibling(h):
        return remote(cand_ref.at[h, other], sib_ref.at[h], h * per, {"col": cpartners[0]})

    def to_far(h, s):
        return remote(mix_ref.at[h, s - 1], far_ref.at[h, s - 1], h * per + s, {"col": cpartners[s]})

    def to_after(h):
        return remote(edge_ref.at[h, 1], halo_ref.at[h, 0], h * per + sides, {"tm": me + 1})

    def from_before(h):
        return remote(edge_ref.at[h, 1], halo_ref.at[h, 0], h * per + sides, {"tm": me - 1})

    def to_before(h):
        return remote(edge_ref.at[h, 0], halo_ref.at[h, 1], h * per + sides + 1, {"tm": me - 1})

    def from_after(h):
        return remote(edge_ref.at[h, 0], halo_ref.at[h, 1], h * per + sides + 1, {"tm": me + 1})

    def give(h):
        return remote(w_ref.at[h, mine], w_ref.at[h, mine], h * per + sides + 2, {"col": cpartners[0]})

    def take(h):
        return remote(w_ref.at[h, other], w_ref.at[h, other], h * per + sides + 2, {"col": cpartners[0]})

    tail_at = chunks * per

    def tail_copy(where):
        return remote(tail_ref, tailhalo_ref, tail_at, {"tm": where})

    def lend(j):
        return remote(moved_hbm.at[j], d_ref.at[blocks + 1 + j], tail_at + 1 + j, {"col": cpartners[0]})

    def give_back(j):
        return remote(o_ref.at[j], back_ref.at[j], tail_at + 1 + MOVED + j, {"col": cpartners[0]})

    if sides:
        for h in range(chunks):
            to_sibling(h).start()

    @pl.when(has_after)
    def _():
        tail_copy(me + 1).start()

    for j in range(MOVED):
        lend(j).start()

    for h in range(chunks):
        if sides:
            to_sibling(h).wait_recv()
            mix_ref[h, 0] = cand_ref[h, mine] + sib_ref[h]
        else:
            mix_ref[h, 0] = cand_ref[h]
        if sides > 1:
            to_far(h, 1).start()

    done = max(sides - 1, 0)

    def meet(h, s):
        to_far(h, s).wait_recv()
        mix_ref[h, s] = mix_ref[h, s - 1] + far_ref[h, s - 1]
        if s + 1 < sides:
            to_far(h, s + 1).start()

    def start_halo(h):
        edge_ref[h, 0] = mix_ref[h, done, :, :taps]
        edge_ref[h, 1] = mix_ref[h, done, :, rows - taps :]

        @pl.when(has_after)
        def _():
            to_after(h).start()

        @pl.when(has_before)
        def _():
            to_before(h).start()

    count_t = rows // taps

    def stacked(x, pieces):
        return jnp.concatenate([x[:, b * taps : (b + 2) * taps] for b in range(pieces)], axis=0)

    def unstacked(x, pieces):
        tall_ = x.shape[0] // pieces
        return jnp.concatenate([x[b * tall_ : (b + 1) * tall_] for b in range(pieces)], axis=1)

    def forward():
        return band_ref[0], band_ref[1]

    def adjoint():
        return band_ref[2], band_ref[3]

    def filter_last():
        @pl.when(has_before)
        def _():
            tail_copy(me - 1).wait_recv()

        @pl.when(jnp.logical_not(has_before))
        def _():
            tailhalo_ref[...] = jnp.zeros_like(tailhalo_ref)

        wide = max(taps, share)
        @pl.loop(0, PANEL // wide)
        def _(j):
            at = pl.ds(pl.multiple_of(j * wide, wide), wide)
            extended = jnp.concatenate([tailhalo_ref[at], last_ref[at]], axis=1)
            y_last = unstacked(dot3(split(stacked(extended, count_t)), forward()), count_t)
            d_ref[blocks, :, at] = y_last.T
            yhi, ylo = split(y_last)
            if chunks == 1:
                whi_ref[1, 0, at] = yhi
                wlo_ref[1, 0, at] = ylo
                return
            for h in range(chunks):
                for d in range(wide // share):
                    to = pl.ds(pl.multiple_of(j * (wide // chunks) + d * part, part), part)
                    rows_of = slice(d * share + h * part, d * share + (h + 1) * part)
                    whi_ref[1, h, to] = yhi[rows_of]
                    wlo_ref[1, h, to] = ylo[rows_of]

    def filter_chunk(h):
        @pl.when(has_before)
        def _():
            from_before(h).wait_recv()

        @pl.when(jnp.logical_not(has_before))
        def _():
            halo_ref[h, 0] = jnp.zeros_like(halo_ref[h, 0])

        @pl.when(has_after)
        def _():
            from_after(h).wait_recv()

        @pl.when(jnp.logical_not(has_after))
        def _():
            halo_ref[h, 1] = jnp.zeros_like(halo_ref[h, 1])

        whole = jnp.concatenate([halo_ref[h, 0], mix_ref[h, done], halo_ref[h, 1]], axis=1)
        y = unstacked(dot3(split(stacked(whole, count_t + 1)), forward()), count_t + 1)
        beyond = lax.broadcasted_iota(i32, y.shape, 1) >= jnp.where(has_after, rows + taps, rows)
        y = jnp.where(beyond, 0.0, y)
        w_ref[h, mine] = unstacked(dot3(split(stacked(y, count_t)), adjoint()), count_t)
        if sides:
            give(h).start()

    def ready_chunk(h):
        if sides:
            take(h).wait_recv()
        whi_ref[0, h], wlo_ref[0, h] = split(w_ref[h])

    def mixed(h):
        for s in range(1, sides):
            meet(h, s)
        start_halo(h)

    early = min(EARLY, count)

    mixed(0)
    filter_last()

    @pl.loop(0, blocks)
    def _(c):
        load(c).wait()

    for j in range(MOVED):
        lend(j).wait_recv()

    def other_order(u):
        return (u % 4) // 3 if levels > 1 else 0

    def bit_of(s, u):
        if s > 1 or levels == 1:
            return bits[s], partners[s]
        swap = other_order(u)
        return (
            bits[s] + swap * (bits[1 - s] - bits[s]),
            partners[s] + swap * (partners[1 - s] - partners[s]),
        )

    def piece(s, u, bit):
        return (u,) + (slice(None),) * (levels - s - 1) + (bit,)

    def copy(s, u):
        src = p_ref if s == 0 else bufs[s - 1]
        bit, partner = bit_of(s, u)
        return pltpu.make_async_remote_copy(
            src_ref=src.at[piece(s, u, 1 - bit)],
            dst_ref=bufs[s].at[u],
            send_sem=send_sem.at[s, u],
            recv_sem=recv_sem.at[s, u],
            device_id={"tm": partner},
            device_id_type=MESH,
        )

    def compute(u):
        h, g = u // count, u % count
        d_at = index_ref[g]
        w_at = jnp.where(d_at == blocks, 1, 0)
        d_block = d_ref[d_at]
        value = dot3((whi_ref[w_at, h], wlo_ref[w_at, h]), split(d_block))
        for i in range(n):
            at = [(i >> s) & 1 for s in reversed(range(levels))]
            rows_of = value[i * part : (i + 1) * part]
            if levels == 1:
                p_ref[(u, *at)] = rows_of
                continue
            first, second = at[-2], at[-1]
            swap = other_order(u)
            p_ref[(u, *at[:-2], first + swap * (second - first), second + swap * (first - second))] = rows_of

    def add(s, u):
        copy(s, u).wait_recv()
        src = p_ref if s == 0 else bufs[s - 1]
        total = bufs[s][u] + src[piece(s, u, bit_of(s, u)[0])]
        if s == levels - 1:
            o_ref[u % count, u // count] = total
            lent = u - (chunks - 1) * count

            @pl.when(jnp.logical_and(lent >= 0, lent < MOVED))
            def _():
                give_back(lent).start()

        else:
            bufs[s][u] = total
            copy(s + 1, u).start()

    def step(i):
        @pl.when(jnp.logical_and(i >= 0, i < units))
        def _():
            compute(i)
            copy(0, i).start()

        for s in range(levels):
            u = i - LAG * (s + 1)

            @pl.when(jnp.logical_and(u >= 0, u < units))
            def _():
                add(s, u)

    @pl.loop(-1, units + LAG * levels)
    def _(i):
        @pl.when(i == -1 if chunks == 1 else jnp.logical_or(i == -1, i == early))
        def _():
            h = jnp.where(i == early, 1, 0) if chunks > 1 else 0
            filter_chunk(h)
            if chunks > 1:

                @pl.when(i == -1)
                def _():
                    mixed(1)

            ready_chunk(h)

        step(i)

    for h in range(chunks):
        if sides:
            to_sibling(h).wait_send()
            give(h).wait_send()
        for s in range(1, sides):
            to_far(h, s).wait_send()

        @pl.when(has_after)
        def _():
            to_after(h).wait_send()

        @pl.when(has_before)
        def _():
            to_before(h).wait_send()

    @pl.when(has_after)
    def _():
        tail_copy(me + 1).wait_send()

    @pl.loop(0, units)
    def _(u):
        for s in range(levels):
            copy(s, u).wait_send()

    for j in range(MOVED):
        lend(j).wait_send()
        give_back(j).wait()
        o_ref[blocks + 1 + j] = back_ref[j]


def place_kernel(epochs, slot_ref, meta_ref, r_ref, o_hbm, o_ref, sem):
    blocks = slot_ref.shape[0]
    jp, end, gram = meta_ref[1], meta_ref[2], meta_ref[3]
    groups = sem.shape[0]
    per = blocks // groups

    def value(at):
        x = r_ref[at]
        return x.reshape(x.shape[0] * x.shape[1], x.shape[2]) / epochs

    def store(q):
        cols = pl.ds(pl.multiple_of(q * per * PANEL, PANEL), per * PANEL)
        return pltpu.make_async_copy(o_ref.at[:, :, cols], o_hbm.at[:, :, cols], sem.at[q])

    @pl.loop(0, groups)
    def _(q):
        for k in range(per):
            b = q * per + k
            cols = pl.ds(pl.multiple_of(b * PANEL, PANEL), PANEL)
            slot = slot_ref[b]
            o_ref[jp, :, cols] = jnp.where(slot >= 0, value(jnp.maximum(slot, 0)), 0.0)
            o_ref[1 - jp, :, cols] = jnp.where(end == b, value(jnp.where(end == b, gram, 0)), 0.0)
        store(q).start()

    @pl.loop(0, groups)
    def _(q):
        store(q).wait()


def vmem():
    return pl.BlockSpec(memory_space=pltpu.VMEM)


def smem():
    return pl.BlockSpec(memory_space=pltpu.SMEM)


def hbm():
    return pl.BlockSpec(memory_space=pl.ANY)


def params(**kw):
    return pltpu.CompilerParams(vmem_limit_bytes=56 * 2**20, **kw)


def summed_rows(count, index, band, cand, last, moved, design, n, groups, cid):
    rows = design.shape[0]
    blocks = design.shape[1] // PANEL
    share = PANEL // n
    levels = n.bit_length() - 1
    sides = groups.bit_length() - 1
    chunks = chunks_of(n)
    part = share // chunks
    tall = PANEL // chunks
    half = tall // 2 if sides else tall
    units = chunks * count
    taps = band.shape[2]
    slots = blocks + 1
    copies = chunks * (sides + 3) + 1 + 2 * MOVED
    return pl.pallas_call(
        functools.partial(rows_kernel, levels, sides, count),
        out_shape=jax.ShapeDtypeStruct((slots + MOVED, chunks, part, PANEL), f32),
        in_specs=[smem(), vmem(), vmem(), vmem(), hbm(), hbm()],
        out_specs=vmem(),
        scratch_shapes=[
            pltpu.VMEM((blocks + 1 + MOVED, rows, PANEL), f32),
            pltpu.VMEM((units,) + (2,) * levels + (part, PANEL), f32),
            pltpu.VMEM((2, chunks, tall, rows), bf16),
            pltpu.VMEM((2, chunks, tall, rows), bf16),
            pltpu.VMEM((chunks, tall, rows), f32),
            pltpu.VMEM((chunks, max(sides, 1), half, rows), f32),
            pltpu.VMEM((chunks, half, rows), f32),
            pltpu.VMEM((chunks, max(sides - 1, 1), half, rows), f32),
            pltpu.VMEM((chunks, 2, half, taps), f32),
            pltpu.VMEM((chunks, 2, half, taps), f32),
            pltpu.VMEM((PANEL, taps), f32),
            pltpu.VMEM((PANEL, taps), f32),
            pltpu.VMEM((MOVED, chunks, part, PANEL), f32),
        ]
        + [pltpu.VMEM((units,) + (2,) * (levels - s - 1) + (part, PANEL), f32) for s in range(levels)]
        + [
            pltpu.SemaphoreType.DMA((blocks,)),
            pltpu.SemaphoreType.DMA((levels, units)),
            pltpu.SemaphoreType.DMA((levels, units)),
            pltpu.SemaphoreType.DMA((copies,)),
            pltpu.SemaphoreType.DMA((copies,)),
        ],
        compiler_params=params(collective_id=cid, has_side_effects=True),
        name=f"rows_{count}",
    )(index, band, cand, last, moved, design)


def shards(design, fir_taps, column_block, panels):
    rows, width = design.shape
    taps = fir_taps.shape[0]
    blocks = width // PANEL
    n = lax.axis_size("tm")
    groups = lax.axis_size("col")
    epochs = rows * n
    chunks = chunks_of(n)
    slots = blocks + 1

    cand, last, band, moved, index, slot, meta = pl.pallas_call(
        functools.partial(prepare_kernel, groups, n),
        out_shape=(
            jax.ShapeDtypeStruct((chunks, PANEL // chunks, rows), f32),
            jax.ShapeDtypeStruct((PANEL, rows), f32),
            jax.ShapeDtypeStruct((4, 2 * taps, taps), bf16),
            jax.ShapeDtypeStruct((MOVED, rows, PANEL), f32),
            jax.ShapeDtypeStruct((slots + 2,), i32),
            jax.ShapeDtypeStruct((blocks,), i32),
            jax.ShapeDtypeStruct((4,), i32),
        ),
        in_specs=[hbm()] * 4,
        out_specs=(vmem(), vmem(), vmem(), hbm(), smem(), smem(), smem()),
        scratch_shapes=[
            pltpu.SMEM(column_block.shape, i32),
            pltpu.SMEM(panels.shape, i32),
            pltpu.VMEM((1, taps), f32),
            pltpu.SMEM((MOVED + 1,), i32),
            pltpu.VMEM((2, rows, PANEL), f32),
            pltpu.SemaphoreType.DMA((5 + MOVED,)),
        ],
        compiler_params=pltpu.CompilerParams(vmem_limit_bytes=60 * 2**20),
        name="prepare",
    )(column_block, panels, fir_taps.reshape(1, taps), design)
    counts = sorted({min(c, slots) for c in range(STEP, slots + STEP, STEP)})

    def branch(order, count, *operands):
        return summed_rows(count, *operands, n, groups, order)

    pick = jnp.clip((meta[0] + STEP - 1) // STEP - 1, 0, len(counts) - 1)
    own_rows = lax.switch(
        pick,
        [functools.partial(branch, i, c) for i, c in enumerate(counts)],
        index, band, cand, last, moved, design,
    )
    return pl.pallas_call(
        functools.partial(place_kernel, epochs),
        out_shape=jax.ShapeDtypeStruct((2, PANEL // n, width), f32),
        in_specs=[smem(), smem(), vmem()],
        out_specs=hbm(),
        scratch_shapes=[pltpu.VMEM((2, PANEL // n, width), f32), pltpu.SemaphoreType.DMA((8 if blocks % 8 == 0 else blocks,))],
        compiler_params=pltpu.CompilerParams(vmem_limit_bytes=8 * 2**20),
        name="place",
    )(slot, meta, own_rows)


def solution(mesh):
    return jax.shard_map(
        shards,
        mesh=mesh,
        in_specs=(P("tm", "col"), P(), P(), P()),
        out_specs=P(None, "tm", "col"),
        check_vma=False,
    )
```
